32 devices in a mesh: region: 4 (over y, x), scen: 8 (over z, core).
Axes of the slice: x: 2, y: 2, z: 4, core: 2. Of those that a mesh axis runs over, the one named last changes fastest.
Arguments:
- start_state: float32 [4, 128, 24, 1024], P('region', 'scen'), may hold values from -6 to 6
- price: float32 [4, 128, 24, 1024], P('region', 'scen'), may hold values from -6 to 6
- demand: float32 [4, 128, 24, 1024], P('region', 'scen'), may hold values from 0.2 to 2
- sens: bfloat16 [4, 1024, 1024], P('region'), as said below
- gen_bus: int32 [4, 512], P('region'), may hold values from 0 to 1023
- gen_cap: float32 [4, 512], P('region'), may hold values from 0.5 to 3
- tie_index: int32 [4, 2, 512], P('region'), may hold values from 0 to 1023, as said below
- tie_len: int32 [4, 2], P('region'), may hold values from 128 to 512, as said below
Outputs:
- final_state: float32 [4, 128, 24, 1024], P('region', 'scen')
- plan: float32 [4, 24, 1024], P('region')
The draws below stay inside these ranges and needn't reach their ends.
Inputs may be any that keep to these rules, and one draw needn't show every extreme that they name: `tie_index`: for each region the two rows together hold each of the 1024 bus numbers exactly once. tie_len[r, 1] equals tie_len[(r + 1) mod 4, 0]; some border has exactly 512 live slots. `sens`: each matrix has a positive diagonal between 0.5 and 2 and off-diagonal entries of order 1 / sqrt(1024).
All inputs are finite; a program needn't handle non-finite values.
Results may differ from the reference program's by a relative error of at most 0.00098.
Values sent between devices are 32-bit elements; how exact they have to be, the bound alone decides.
A program may use at most 64 MiB of HBM per device.

```python
import math
import jax
import jax.numpy as jnp
from jax import lax

NB = 1024
TIE = 512
H = 24
G = 512
SWEEPS = 2
STEPS = 3
REGIONS = 4
SCEN = 128


def draw_sens(key, part):
    key_diag, key_off = jax.random.split(key, 2)
    diagonal = jnp.exp(jax.random.uniform(key_diag, (REGIONS, NB), jnp.float32, math.log(0.5), math.log(2.0)))
    off_part = jax.random.normal(key_off, (REGIONS, NB, NB), jnp.float32) * 0.5 / NB ** 0.5
    identity = jnp.eye(NB, dtype=jnp.float32)
    return (off_part * (1.0 - identity) + diagonal[:, :, None] * identity).astype(jnp.bfloat16)


def draw_tie_index(key, part):
    region_keys = jax.random.split(key, REGIONS)

    def one_region(region_key):
        return jax.random.permutation(region_key, NB).reshape(2, NB // 2)
    return jax.vmap(one_region)(region_keys).astype(jnp.int32)


def draw_tie_len(key, part):
    key_len, key_place = jax.random.split(key)
    border = jax.random.randint(key_len, (REGIONS,), TIE // 4, TIE + 1)
    chosen = jax.random.randint(key_place, (), 0, REGIONS)
    border = jnp.where(jnp.arange(REGIONS) == chosen, TIE, border)
    return jnp.stack([jnp.roll(border, 1), border], axis=1).astype(jnp.int32)


def set_ends(drawn, stream_key, low, top_value):
    longest = drawn.shape.index(max(drawn.shape))
    spots = []
    for shift in (0, 1):
        where = [jax.random.randint(jax.random.fold_in(stream_key, axis), (), 0, length) for axis, length in enumerate(drawn.shape)]
        where[longest] = (where[longest] + shift) % drawn.shape[longest]
        spots.append(tuple(where))
    return drawn.at[spots[0]].set(low).at[spots[1]].set(top_value)


def block_levels(key, extent, cuts, low, top_value):
    loudness = 1.0
    for position, parts in cuts:
        draws = jax.random.uniform(jax.random.fold_in(jax.random.fold_in(key, 6), position), (parts,), jnp.float32, low / len(cuts), top_value / len(cuts))
        loudness = loudness * jnp.repeat(jnp.exp(draws), extent[position] // parts).reshape((-1,) + (1,) * (len(extent) - 1 - position))
    return loudness


def normal_values(rng, extent, width, limit, pieces=(), kind=jnp.bfloat16):
    array = width * jax.random.normal(rng, extent, jnp.float32)
    if pieces:
        array = array * block_levels(rng, extent, pieces, -0.22, 0.18)
    return jnp.clip(array, -limit, limit).astype(kind)


def setup_inputs(seed: int = 0) -> dict:
    seeds = jax.random.split(jax.random.key(seed), 9)
    start_state = normal_values(seeds[0], (REGIONS, SCEN, H, NB), 1.0, 6.0, ((0, 4), (1, 8)), jnp.float32)
    price = normal_values(seeds[1], (REGIONS, SCEN, H, NB), 1.0, 6.0, ((0, 4), (1, 8)), jnp.float32)
    demand = jnp.clip(jnp.exp(math.log(2.0) - 2.3025851 * jax.random.uniform(seeds[2], (REGIONS, SCEN, H, NB), jnp.float32) ** block_levels(seeds[2], (REGIONS, SCEN, H, NB), ((0, 4), (1, 8)), -0.2, 0.2)), 0.2, 2.0)
    sens = draw_sens(jax.random.fold_in(seeds[8], 71), 0)
    gen_bus = set_ends(jax.random.randint(seeds[4], (REGIONS, G), 0, NB), jax.random.fold_in(seeds[4], 1), 0, NB - 1).astype(jnp.int32)
    gen_cap = jnp.clip(jnp.exp(math.log(3.0) - 1.7917595 * jax.random.uniform(seeds[5], (REGIONS, G), jnp.float32) ** block_levels(seeds[5], (REGIONS, G), ((0, 4),), -0.2, 0.2)), 0.5, 3.0)
    tie_index = draw_tie_index(jax.random.fold_in(seeds[8], 71), 0)
    tie_len = draw_tie_len(jax.random.fold_in(seeds[8], 71), 0)
    return {"start_state": start_state, "price": price, "demand": demand, "sens": sens, "gen_bus": gen_bus, "gen_cap": gen_cap, "tie_index": tie_index, "tie_len": tie_len}


step_rate = 0.3
tie_weight = 1.0
day_weight = 0.5


def pick_blocks(region_state, indices):
    return jnp.stack([region_state[..., indices[0]], region_state[..., indices[1]]])


def place_blocks(values, indices):
    placed = jnp.zeros(values.shape[1:3] + (NB,), jnp.float32)
    placed = placed.at[..., indices[0]].set(values[0])
    return placed.at[..., indices[1]].set(values[1])


def place_mask(live, indices):
    placed = jnp.zeros((NB,), jnp.float32)
    return placed.at[indices[0]].set(live[0]).at[indices[1]].set(live[1])


def add_caps(buses, capacity):
    return jnp.zeros((NB,), jnp.float32).at[buses].add(capacity)


def descend(items):
    state, price_part, demand_part, matrix, target, tie_mask, plan, day_dual, upper = items
    for repeat in range(STEPS):
        rounded = state.reshape(-1, NB).astype(jnp.bfloat16)
        slope = jnp.dot(rounded, matrix, preferred_element_type=jnp.float32).reshape(state.shape)
        slope = slope + price_part + tie_weight * tie_mask * (state - target) + day_weight * (state - plan + day_dual)
        state = jnp.clip(state - step_rate * slope, -demand_part, upper)
    return state


def reference(start_state, price, demand, sens, gen_bus, gen_cap, tie_index, tie_len):
    state = start_state
    live = (jnp.arange(TIE, dtype=jnp.int32)[None, None, :] < tie_len[:, :, None]).astype(jnp.float32)
    upper = jax.vmap(add_caps)(gen_bus, gen_cap)
    tie_mask = jax.vmap(place_mask)(live, tie_index)
    tie_dual = jnp.zeros((REGIONS, 2, SCEN, H, TIE), jnp.float32)
    day_dual = jnp.zeros_like(state)
    plan = jnp.zeros((REGIONS, H, NB), jnp.float32)
    for sweep in range(SWEEPS):
        blocks = jax.vmap(pick_blocks)(state, tie_index)
        from_left = jnp.roll(blocks[:, 1], 1, axis=0)
        from_right = jnp.roll(blocks[:, 0], -1, axis=0)
        theirs = jnp.stack([from_left, from_right], axis=1)
        middle = 0.5 * (blocks + theirs)
        tie_dual = tie_dual + blocks - middle
        target_blocks = (middle - tie_dual) * live[:, :, None, None, :]
        target = jax.vmap(place_blocks)(target_blocks, tie_index)
        plan = jnp.sum(state + day_dual, axis=1) / SCEN
        day_dual = day_dual + state - plan[:, None]
        state = lax.map(descend, (state, price, demand, sens, target, tie_mask, plan, day_dual, upper))
    return state, plan
```

```python
import functools
import jax
import jax.numpy as jnp
from jax import lax
from jax.experimental import pallas as pl
from jax.experimental.pallas import tpu as pltpu
from jax.sharding import PartitionSpec as P

SWEEPS = 2
STEPS = 3
SUB = 8
LANES = 128
TILE = 256


step_rate = 0.3
tie_weight = 1.0
day_weight = 0.5

MESH = pl.DeviceIdType.MESH


def kernel(
    total_scen, regions, peers,
    s0_hbm, price_hbm, demand_hbm, sens_hbm, gen_bus, gen_cap, tie_index, tie_len,
    out_hbm, plan_out,
    st, dd, pr, dm, mat, pick, place, mrow, arow, urow, split, rb, kk,
    snd, rcv, pbuf,
    in_sem, mat_sem, out_sem, send_sem, recv_sem, psend_sem, precv_sem,
):
    chunks, scens, _, buses = st.shape
    slots = tie_index.shape[1]
    rows = scens * SUB
    tiles = buses // TILE
    me = lax.axis_index("scen")
    reg = lax.axis_index("region")
    up = lax.rem(reg + 1, regions)
    down = lax.rem(reg + regions - 1, regions)

    def load(kind, source, target, c):
        return pltpu.make_async_copy(source.at[:, pl.ds(pl.multiple_of(c * SUB, SUB), SUB), :], target.at[c], in_sem.at[kind, c])

    for c in range(chunks):
        load(0, s0_hbm, st, c).start()

    barrier = pltpu.get_barrier_semaphore()
    for other in (up, down):
        pl.semaphore_signal(barrier, inc=1, device_id={"region": other}, device_id_type=MESH)
    for d in range(1, peers):
        pl.semaphore_signal(barrier, inc=1, device_id={"scen": lax.rem(me + d, peers)}, device_id_type=MESH)

    mat_copy = pltpu.make_async_copy(sens_hbm, mat, mat_sem)
    mat_copy.start()
    for c in range(chunks):
        load(1, price_hbm, pr, c).start()
        load(2, demand_hbm, dm, c).start()

    def one_hot(hit):
        return jnp.where(hit, 1.0, 0.0)

    for k in range(2):
        wanted = jnp.broadcast_to(tie_index[k:k + 1, :], (LANES, slots))
        for b in range(buses // LANES):
            ids = lax.broadcasted_iota(jnp.int32, (LANES, slots), 0) + b * LANES
            pick[b * LANES:(b + 1) * LANES, k * slots:(k + 1) * slots] = one_hot(ids == wanted).astype(jnp.bfloat16)

    pl.semaphore_wait(barrier, 2 + peers - 1)

    def tie_copy(u, k):
        return pltpu.make_async_remote_copy(
            src_ref=snd.at[u, k], dst_ref=rcv.at[u, 1 - k],
            send_sem=send_sem.at[u, k], recv_sem=recv_sem.at[u, 1 - k],
            device_id={"region": (down, up)[k]}, device_id_type=MESH,
        )

    def plan_copy(u, d):
        return pltpu.make_async_remote_copy(
            src_ref=pbuf.at[u, me], dst_ref=pbuf.at[u, me],
            send_sem=psend_sem.at[u, d], recv_sem=precv_sem.at[u, me],
            device_id={"scen": lax.rem(me + d, peers)}, device_id_type=MESH,
        )

    def plan_arrival(u, d):
        src = lax.rem(me + d, peers)
        return pltpu.make_async_remote_copy(
            src_ref=pbuf.at[u, src], dst_ref=pbuf.at[u, src],
            send_sem=psend_sem.at[u, d], recv_sem=precv_sem.at[u, src],
            device_id={"scen": src}, device_id_type=MESH,
        )

    def put_split(value, at, width):
        high = value.astype(jnp.bfloat16)
        split[:rows, at:at + width] = high
        split[rows:, at:at + width] = (value - high.astype(jnp.float32)).astype(jnp.bfloat16)

    def select(weights, n):
        both = jnp.dot(split[...], weights[:, n * TILE:(n + 1) * TILE], preferred_element_type=jnp.float32)
        return both[:rows] + both[rows:]

    def send_ties(u, c):
        for n in range(tiles):
            put_split(st[c, :, :, n * TILE:(n + 1) * TILE].reshape(rows, TILE), n * TILE, TILE)
        per_side = slots // TILE
        for n in range(tiles):
            k, at = n // per_side, n % per_side
            snd[u, k, :, at * TILE:(at + 1) * TILE] = select(pick, n)
            if at == per_side - 1:
                tie_copy(u, k).start()

    def send_plan(u):
        for d in range(1, peers):
            plan_copy(u, d).start()

    def start_chunk(c, carry):
        load(0, s0_hbm, st, c).wait()
        send_ties(c, c)
        pbuf[c, me] = jnp.sum(st[c], axis=0)
        send_plan(c)
        return carry

    lax.fori_loop(0, chunks, start_chunk, 0)

    for k in range(2):
        column = jnp.transpose(jnp.broadcast_to(tie_index[k:k + 1, :].astype(jnp.float32), (LANES, slots))).astype(jnp.int32)
        alive = lax.broadcasted_iota(jnp.int32, (slots, LANES), 0) < tie_len[0, k]
        for b in range(buses // LANES):
            ids = lax.broadcasted_iota(jnp.int32, (slots, LANES), 1) + b * LANES
            hot = one_hot((ids == column) & alive)
            place[k * slots:(k + 1) * slots, b * LANES:(b + 1) * LANES] = hot.astype(jnp.bfloat16)
            part = jnp.broadcast_to(jnp.sum(hot, axis=0, keepdims=True), (SUB, LANES))
            if k == 0:
                mrow[:, b * LANES:(b + 1) * LANES] = part
            else:
                mrow[:, b * LANES:(b + 1) * LANES] += part
    arow[...] = 1.0 - step_rate * (tie_weight * mrow[...] + day_weight)
    gens = gen_bus.shape[1]
    column = jnp.transpose(jnp.broadcast_to(gen_bus[...].astype(jnp.float32), (LANES, gens))).astype(jnp.int32)
    caps = jnp.transpose(jnp.broadcast_to(gen_cap[...], (LANES, gens)))
    for b in range(buses // LANES):
        ids = lax.broadcasted_iota(jnp.int32, (gens, LANES), 1) + b * LANES
        part = jnp.sum(jnp.where(ids == column, caps, 0.0), axis=0, keepdims=True)
        urow[:, b * LANES:(b + 1) * LANES] = jnp.broadcast_to(part, (SUB, LANES))
    mat_copy.wait()

    def receive(sweep, u, c):
        for d in range(1, peers):
            plan_arrival(u, d).wait_recv()
        plan = pbuf[u, 0]
        for src in range(1, peers):
            plan = plan + pbuf[u, src]
        plan = plan / total_scen
        if sweep == SWEEPS - 1:
            plan_out[c] = plan
        for k in range(2):
            tie_copy(u, 1 - k).wait_recv()
            put_split(rcv[u, k], k * slots, slots)
        for n in range(tiles):
            cols = slice(n * TILE, (n + 1) * TILE)
            theirs = select(place, n).reshape(scens, SUB, TILE)
            now = st[c, :, :, cols]
            day = plan[:, cols]
            base = pr[c, :, :, cols]
            if sweep == 0:
                dual = now - day
                dd[c, :, :, cols] = dual
                pr[c, :, :, cols] = base + (0.5 * tie_weight) * (mrow[:, cols] * now - theirs)
            else:
                dual = dd[c, :, :, cols] + now - day
            kk[:, :, cols] = step_rate * (base - tie_weight * theirs + day_weight * (dual - day))
            rb[0, :, cols] = now.reshape(rows, TILE).astype(jnp.bfloat16)

    def descend(c):
        for step in range(STEPS):
            for n in range(tiles):
                cols = slice(n * TILE, (n + 1) * TILE)
                slope = jnp.dot(rb[step % 2], mat[:, cols], preferred_element_type=jnp.float32).reshape(scens, SUB, TILE)
                new = arow[:, cols] * st[c, :, :, cols] - step_rate * slope - kk[:, :, cols]
                new = jnp.minimum(jnp.maximum(new, -dm[c, :, :, cols]), urow[:, cols])
                st[c, :, :, cols] = new
                if step < STEPS - 1:
                    rb[(step + 1) % 2, :, cols] = new.reshape(rows, TILE).astype(jnp.bfloat16)

    def first_sweep(c, carry):
        load(1, price_hbm, pr, c).wait()
        load(2, demand_hbm, dm, c).wait()
        receive(0, c, c)
        descend(c)
        send_ties(chunks + c, c)
        pbuf[chunks + c, me] = jnp.sum(st[c] + dd[c], axis=0)
        send_plan(chunks + c)
        return carry

    lax.fori_loop(0, chunks, first_sweep, 0)

    def store(c):
        return pltpu.make_async_copy(st.at[c], out_hbm.at[:, pl.ds(pl.multiple_of(c * SUB, SUB), SUB), :], out_sem.at[c])

    def last_sweep(c, carry):
        receive(1, chunks + c, c)
        descend(c)
        store(c).start()
        return carry

    lax.fori_loop(0, chunks, last_sweep, 0)

    def finish(u, carry):
        for k in range(2):
            tie_copy(u, k).wait_send()
        for d in range(1, peers):
            plan_copy(u, d).wait_send()
        return carry

    lax.fori_loop(0, SWEEPS * chunks, finish, 0)
    for c in range(chunks):
        store(c).wait()


def body(start_state, price, demand, sens, gen_bus, gen_cap, tie_index, tie_len):
    _, scens, hours, buses = start_state.shape
    slots = tie_index.shape[2]
    peers = lax.axis_size("scen")
    regions = lax.axis_size("region")
    chunks = hours // SUB
    rows = scens * SUB
    f32, bf16 = jnp.float32, jnp.bfloat16
    resident = pl.BlockSpec(memory_space=pltpu.VMEM)
    anywhere = pl.BlockSpec(memory_space=pl.ANY)
    whole = pltpu.VMEM((chunks, scens, SUB, buses), f32)
    final, plan = pl.pallas_call(
        functools.partial(kernel, scens * peers, regions, peers),
        out_shape=(
            jax.ShapeDtypeStruct((scens, hours, buses), f32),
            jax.ShapeDtypeStruct((chunks, SUB, buses), f32),
        ),
        in_specs=[anywhere] * 4 + [resident] * 3 + [pl.BlockSpec(memory_space=pltpu.SMEM)],
        out_specs=(anywhere, resident),
        scratch_shapes=[
            whole, whole, whole, whole,
            pltpu.VMEM((buses, buses), bf16),
            pltpu.VMEM((buses, 2 * slots), bf16),
            pltpu.VMEM((2 * slots, buses), bf16),
            pltpu.VMEM((SUB, buses), f32),
            pltpu.VMEM((SUB, buses), f32),
            pltpu.VMEM((SUB, buses), f32),
            pltpu.VMEM((2 * rows, buses), bf16),
            pltpu.VMEM((2, rows, buses), bf16),
            pltpu.VMEM((scens, SUB, buses), f32),
            pltpu.VMEM((SWEEPS * chunks, 2, rows, slots), f32),
            pltpu.VMEM((SWEEPS * chunks, 2, rows, slots), f32),
            pltpu.VMEM((SWEEPS * chunks, peers, SUB, buses), f32),
            pltpu.SemaphoreType.DMA((3, chunks)),
            pltpu.SemaphoreType.DMA,
            pltpu.SemaphoreType.DMA((chunks,)),
            pltpu.SemaphoreType.DMA((SWEEPS * chunks, 2)),
            pltpu.SemaphoreType.DMA((SWEEPS * chunks, 2)),
            pltpu.SemaphoreType.DMA((SWEEPS * chunks, peers)),
            pltpu.SemaphoreType.DMA((SWEEPS * chunks, peers)),
        ],
        compiler_params=pltpu.CompilerParams(collective_id=0, has_side_effects=True),
        name="dispatch",
    )(start_state[0], price[0], demand[0], sens[0], gen_bus, gen_cap, tie_index[0], tie_len)
    return (final[None], plan.reshape(1, hours, buses))


def solution(mesh):
    in_specs = (
        P("region", "scen", None, None),
        P("region", "scen", None, None),
        P("region", "scen", None, None),
        P("region", None, None),
        P("region", None),
        P("region", None),
        P("region", None, None),
        P("region", None),
    )
    out_specs = (P("region", "scen", None, None), P("region", None, None))
    return jax.shard_map(body, mesh=mesh, in_specs=in_specs, out_specs=out_specs, check_vma=False)
```

```python
import functools
import jax
import jax.numpy as jnp
from jax import lax
from jax.experimental import pallas as pl
from jax.experimental.pallas import tpu as pltpu
from jax.sharding import PartitionSpec as P

SWEEPS = 2
STEPS = 3
SUB = 8
LANES = 128
TILE = 256
PARTS = 2


step_rate = 0.3
tie_weight = 1.0
day_weight = 0.5

MESH = pl.DeviceIdType.MESH


def kernel(
    total_scen, regions, peers,
    s0_hbm, price_hbm, demand_hbm, sens_hbm, gen_bus, gen_cap, tie_index, tie_len,
    out, plan_out,
    st, dd, pr, dm, mat, pick, place, mrow, arow, urow, split, rb, kk, first,
    snd, rcv, pbuf,
    in_sem, mat_sem, send_sem, recv_sem, psend_sem, precv_sem,
):
    chunks, scens, _, buses = st.shape
    slots = tie_index.shape[1]
    rows = scens * SUB
    tiles = buses // TILE
    me = lax.axis_index("scen")
    reg = lax.axis_index("region")
    up = lax.rem(reg + 1, regions)
    down = lax.rem(reg + regions - 1, regions)

    def load(kind, source, target, c):
        return pltpu.make_async_copy(source.at[:, pl.ds(pl.multiple_of(c * SUB, SUB), SUB), :], target.at[c], in_sem.at[kind, c])

    for c in range(chunks):
        load(0, s0_hbm, st, c).start()

    barrier = pltpu.get_barrier_semaphore()
    for other in (up, down):
        pl.semaphore_signal(barrier, inc=1, device_id={"region": other}, device_id_type=MESH)
    for d in range(1, peers):
        pl.semaphore_signal(barrier, inc=1, device_id={"scen": lax.rem(me + d, peers)}, device_id_type=MESH)

    mat_copy = pltpu.make_async_copy(sens_hbm, mat, mat_sem)
    mat_copy.start()
    for c in range(chunks):
        load(1, price_hbm, pr, c).start()
        load(2, demand_hbm, dm, c).start()

    def one_hot(hit):
        return jnp.where(hit, 1.0, 0.0)

    def build_pick(k):
        wanted = jnp.broadcast_to(tie_index[k:k + 1, :], (LANES, slots))
        for b in range(buses // LANES):
            ids = lax.broadcasted_iota(jnp.int32, (LANES, slots), 0) + b * LANES
            pick[b * LANES:(b + 1) * LANES, k * slots:(k + 1) * slots] = one_hot(ids == wanted).astype(jnp.bfloat16)

    build_pick(0)
    pl.semaphore_wait(barrier, 2 + peers - 1)

    def tie_copy(u, k, part):
        span = pl.ds(part * (rows // PARTS), rows // PARTS)
        return pltpu.make_async_remote_copy(
            src_ref=snd.at[u, k, span], dst_ref=rcv.at[u, 1 - k, span],
            send_sem=send_sem.at[u, k, part], recv_sem=recv_sem.at[u, 1 - k, part],
            device_id={"region": (down, up)[k]}, device_id_type=MESH,
        )

    def plan_copy(u, d):
        return pltpu.make_async_remote_copy(
            src_ref=pbuf.at[u, me], dst_ref=pbuf.at[u, me],
            send_sem=psend_sem.at[u, d], recv_sem=precv_sem.at[u, me],
            device_id={"scen": lax.rem(me + d, peers)}, device_id_type=MESH,
        )

    def plan_arrival(u, d):
        src = lax.rem(me + d, peers)
        return pltpu.make_async_remote_copy(
            src_ref=pbuf.at[u, src], dst_ref=pbuf.at[u, src],
            send_sem=psend_sem.at[u, d], recv_sem=precv_sem.at[u, src],
            device_id={"scen": src}, device_id_type=MESH,
        )

    def put_split(value, at, width):
        count = value.shape[0]
        high = value.astype(jnp.bfloat16)
        split[:count, at:at + width] = high
        split[count:2 * count, at:at + width] = (value - high.astype(jnp.float32)).astype(jnp.bfloat16)

    def select(weights, n, count):
        both = jnp.dot(split[:2 * count], weights[:, n * TILE:(n + 1) * TILE], preferred_element_type=jnp.float32)
        return both[:count] + both[count:]

    per_side = slots // TILE

    def split_state(c):
        for n in range(tiles):
            put_split(st[c, :, :, n * TILE:(n + 1) * TILE].reshape(rows, TILE), n * TILE, TILE)

    def gather_ties(u, k):
        for at in range(per_side):
            snd[u, k, :, at * TILE:(at + 1) * TILE] = select(pick, k * per_side + at, rows)

    def send_ties(u, sides):
        for part in range(PARTS):
            for k in sides:
                tie_copy(u, k, part).start()

    def send_plan(u):
        for d in range(1, peers):
            plan_copy(u, d).start()

    def start_chunk(c, peeled):
        load(0, s0_hbm, st, c).wait()
        split_state(c)
        for k in range(2):
            if k == 1 and peeled:
                build_pick(1)
            gather_ties(c, k)
            send_ties(c, (k,))
        pbuf[c, me] = jnp.sum(st[c], axis=0)
        send_plan(c)

    start_chunk(0, True)
    pl.loop(1, chunks)(lambda c: start_chunk(c, False))

    for k in range(2):
        column = jnp.transpose(jnp.broadcast_to(tie_index[k:k + 1, :].astype(jnp.float32), (LANES, slots))).astype(jnp.int32)
        alive = lax.broadcasted_iota(jnp.int32, (slots, LANES), 0) < tie_len[0, k]
        for b in range(buses // LANES):
            ids = lax.broadcasted_iota(jnp.int32, (slots, LANES), 1) + b * LANES
            hot = one_hot((ids == column) & alive)
            place[k * slots:(k + 1) * slots, b * LANES:(b + 1) * LANES] = hot.astype(jnp.bfloat16)
            part = jnp.broadcast_to(jnp.sum(hot, axis=0, keepdims=True), (SUB, LANES))
            if k == 0:
                mrow[:, b * LANES:(b + 1) * LANES] = part
            else:
                mrow[:, b * LANES:(b + 1) * LANES] += part
    arow[...] = 1.0 - step_rate * (tie_weight * mrow[...] + day_weight)
    gens = gen_bus.shape[1]
    column = jnp.transpose(jnp.broadcast_to(gen_bus[...].astype(jnp.float32), (LANES, gens))).astype(jnp.int32)
    caps = jnp.transpose(jnp.broadcast_to(gen_cap[...], (LANES, gens)))
    for b in range(buses // LANES):
        ids = lax.broadcasted_iota(jnp.int32, (gens, LANES), 1) + b * LANES
        part = jnp.sum(jnp.where(ids == column, caps, 0.0), axis=0, keepdims=True)
        urow[:, b * LANES:(b + 1) * LANES] = jnp.broadcast_to(part, (SUB, LANES))
    mat_copy.wait()

    def prepare(sweep, u, c):
        for d in range(1, peers):
            plan_arrival(u, d).wait_recv()
        plan = pbuf[u, 0]
        for src in range(1, peers):
            plan = plan + pbuf[u, src]
        plan = plan / total_scen
        if sweep == SWEEPS - 1:
            plan_out[c] = plan
        for n in range(tiles):
            cols = slice(n * TILE, (n + 1) * TILE)
            now = st[c, :, :, cols]
            day = plan[:, cols]
            base = pr[c, :, :, cols]
            if sweep == 0:
                dual = now - day
                dd[c, :, :, cols] = dual
                pr[c, :, :, cols] = base + (0.5 * tie_weight) * mrow[:, cols] * now
            else:
                dual = dd[c, :, :, cols] + now - day
            kk[:, :, cols] = step_rate * (base + day_weight * (dual - day))
            rb[0, :, cols] = now.reshape(rows, TILE).astype(jnp.bfloat16)
        for n in range(tiles):
            cols = slice(n * TILE, (n + 1) * TILE)
            slope = jnp.dot(rb[0], mat[:, cols], preferred_element_type=jnp.float32).reshape(scens, SUB, TILE)
            first[:, :, cols] = arow[:, cols] * st[c, :, :, cols] - step_rate * slope - kk[:, :, cols]

    def descend(sweep, u, c, parts):
        count = rows // PARTS * len(parts)
        lines = slice(parts[0] * (rows // PARTS), parts[0] * (rows // PARTS) + count)
        some = slice(lines.start // SUB, lines.stop // SUB)
        for k in range(2):
            for part in parts:
                tie_copy(u, 1 - k, part).wait_recv()
            put_split(rcv[u, k, lines], k * slots, slots)

        def advance(n, new, step):
            cols = slice(n * TILE, (n + 1) * TILE)
            new = jnp.minimum(jnp.maximum(new, -dm[c, some, :, cols]), urow[:, cols])
            if step < STEPS - 1:
                rb[(step + 1) % 2, lines, cols] = new.reshape(count, TILE).astype(jnp.bfloat16)
            if sweep == SWEEPS - 1 and step == STEPS - 1:
                out[some, pl.ds(pl.multiple_of(c * SUB, SUB), SUB), cols] = new
            else:
                st[c, some, :, cols] = new

        for n in range(tiles):
            cols = slice(n * TILE, (n + 1) * TILE)
            theirs = select(place, n, count).reshape(count // SUB, SUB, TILE)
            if sweep == 0:
                pr[c, some, :, cols] -= (0.5 * tie_weight) * theirs
            pull = (step_rate * tie_weight) * theirs
            kk[some, :, cols] -= pull
            advance(n, first[some, :, cols] + pull, 0)
        for step in range(1, STEPS):
            for n in range(tiles):
                cols = slice(n * TILE, (n + 1) * TILE)
                slope = jnp.dot(rb[step % 2, lines], mat[:, cols], preferred_element_type=jnp.float32).reshape(count // SUB, SUB, TILE)
                advance(n, arow[:, cols] * st[c, some, :, cols] - step_rate * slope - kk[some, :, cols], step)

    every = tuple(range(PARTS))

    @pl.loop(0, chunks)
    def first_sweep(c):
        load(1, price_hbm, pr, c).wait()
        load(2, demand_hbm, dm, c).wait()
        prepare(0, c, c)
        descend(0, c, c, every)
        u = chunks + c
        pbuf[u, me] = jnp.sum(st[c] + dd[c], axis=0)
        send_plan(u)
        split_state(c)
        for k in range(2):
            gather_ties(u, k)
        send_ties(u, (0, 1))

    @pl.loop(0, chunks - 1)
    def last_sweep(c):
        prepare(1, chunks + c, c)
        descend(1, chunks + c, c, every)

    prepare(1, 2 * chunks - 1, chunks - 1)
    for part in every:
        descend(1, 2 * chunks - 1, chunks - 1, (part,))

    def finish(u, carry):
        for k in range(2):
            for part in every:
                tie_copy(u, k, part).wait_send()
        for d in range(1, peers):
            plan_copy(u, d).wait_send()
        return carry

    lax.fori_loop(0, SWEEPS * chunks, finish, 0)


def body(start_state, price, demand, sens, gen_bus, gen_cap, tie_index, tie_len):
    _, scens, hours, buses = start_state.shape
    slots = tie_index.shape[2]
    peers = lax.axis_size("scen")
    regions = lax.axis_size("region")
    chunks = hours // SUB
    rows = scens * SUB
    f32, bf16 = jnp.float32, jnp.bfloat16
    resident = pl.BlockSpec(memory_space=pltpu.VMEM)
    anywhere = pl.BlockSpec(memory_space=pl.ANY)
    whole = pltpu.VMEM((chunks, scens, SUB, buses), f32)
    final, plan = pl.pallas_call(
        functools.partial(kernel, scens * peers, regions, peers),
        out_shape=(
            pltpu.VMEM((scens, hours, buses), f32),
            pltpu.VMEM((chunks, SUB, buses), f32),
        ),
        in_specs=[anywhere] * 4 + [resident] * 3 + [pl.BlockSpec(memory_space=pltpu.SMEM)],
        out_specs=(resident, resident),
        scratch_shapes=[
            whole, whole, whole, whole,
            pltpu.VMEM((buses, buses), bf16),
            pltpu.VMEM((buses, 2 * slots), bf16),
            pltpu.VMEM((2 * slots, buses), bf16),
            pltpu.VMEM((SUB, buses), f32),
            pltpu.VMEM((SUB, buses), f32),
            pltpu.VMEM((SUB, buses), f32),
            pltpu.VMEM((2 * rows, buses), bf16),
            pltpu.VMEM((2, rows, buses), bf16),
            pltpu.VMEM((scens, SUB, buses), f32),
            pltpu.VMEM((scens, SUB, buses), f32),
            pltpu.VMEM((SWEEPS * chunks, 2, rows, slots), f32),
            pltpu.VMEM((SWEEPS * chunks, 2, rows, slots), f32),
            pltpu.VMEM((SWEEPS * chunks, peers, SUB, buses), f32),
            pltpu.SemaphoreType.DMA((3, chunks)),
            pltpu.SemaphoreType.DMA,
            pltpu.SemaphoreType.DMA((SWEEPS * chunks, 2, PARTS)),
            pltpu.SemaphoreType.DMA((SWEEPS * chunks, 2, PARTS)),
            pltpu.SemaphoreType.DMA((SWEEPS * chunks, peers)),
            pltpu.SemaphoreType.DMA((SWEEPS * chunks, peers)),
        ],
        compiler_params=pltpu.CompilerParams(collective_id=0, has_side_effects=True),
        name="dispatch",
    )(start_state[0], price[0], demand[0], sens[0], gen_bus, gen_cap, tie_index[0], tie_len)
    return (final[None], plan.reshape(1, hours, buses))


def solution(mesh):
    in_specs = (
        P("region", "scen", None, None),
        P("region", "scen", None, None),
        P("region", "scen", None, None),
        P("region", None, None),
        P("region", None),
        P("region", None),
        P("region", None, None),
        P("region", None),
    )
    out_specs = (P("region", "scen", None, None), P("region", None, None))
    return jax.shard_map(body, mesh=mesh, in_specs=in_specs, out_specs=out_specs, check_vma=False)
```

```python
import functools
import jax
import jax.numpy as jnp
from jax import lax
from jax.experimental import pallas as pl
from jax.experimental.pallas import tpu as pltpu
from jax.sharding import PartitionSpec as P

SWEEPS = 2
STEPS = 3
SUB = 8
LANES = 128
TILE = 256
PARTS = 2


step_rate = 0.3
tie_weight = 1.0
day_weight = 0.5

MESH = pl.DeviceIdType.MESH


def kernel(
    total_scen, regions, peers,
    s0_hbm, price_hbm, demand_hbm, sens_hbm, gen_bus, gen_cap, tie_index, tie_len,
    out, plan_out,
    st, dd, pr, dm, mat, pick, place, mrow, arow, urow, split, rb, kk, first,
    snd, rcv, pbuf,
    token, in_sem, mat_sem, send_sem, recv_sem, psend_sem, precv_sem,
):
    chunks, scens, _, buses = st.shape
    slots = tie_index.shape[1]
    rows = scens * SUB
    tiles = buses // TILE
    me = lax.axis_index("scen")
    reg = lax.axis_index("region")
    up = lax.rem(reg + 1, regions)
    down = lax.rem(reg + regions - 1, regions)

    def load(kind, source, target, c):
        return pltpu.make_async_copy(source.at[:, pl.ds(pl.multiple_of(c * SUB, SUB), SUB), :], target.at[c], in_sem.at[kind, c])

    for c in range(chunks):
        load(0, s0_hbm, st, c).start()

    barrier = pltpu.get_barrier_semaphore()
    for other in (up, down):
        pl.semaphore_signal(barrier, inc=1, device_id={"region": other}, device_id_type=MESH)
    half = lax.rem(me, 2)
    place_z = lax.div(me, 2)
    last_z = peers // 2 - 1
    lower, higher = {"scen": me - 2}, {"scen": me + 2}
    pl.semaphore_signal(barrier, inc=1, device_id={"scen": me + 1 - 2 * half}, device_id_type=MESH)

    @pl.when(place_z > 0)
    def _():
        pl.semaphore_signal(barrier, inc=1, device_id=lower, device_id_type=MESH)

    @pl.when(place_z < last_z)
    def _():
        pl.semaphore_signal(barrier, inc=1, device_id=higher, device_id_type=MESH)


    mat_copy = pltpu.make_async_copy(sens_hbm, mat, mat_sem)
    mat_copy.start()
    for c in range(chunks):
        load(1, price_hbm, pr, c).start()
        load(2, demand_hbm, dm, c).start()

    def one_hot(hit):
        return jnp.where(hit, 1.0, 0.0)

    def build_pick(k):
        wanted = jnp.broadcast_to(tie_index[k:k + 1, :], (LANES, slots))
        for b in range(buses // LANES):
            ids = lax.broadcasted_iota(jnp.int32, (LANES, slots), 0) + b * LANES
            pick[b * LANES:(b + 1) * LANES, k * slots:(k + 1) * slots] = one_hot(ids == wanted).astype(jnp.bfloat16)

    build_pick(0)
    def tie_copy(u, k, part):
        span = pl.ds(part * (rows // PARTS), rows // PARTS)
        return pltpu.make_async_remote_copy(
            src_ref=snd.at[u, k, span], dst_ref=rcv.at[u, 1 - k, span],
            send_sem=send_sem.at[u, k, part], recv_sem=recv_sem.at[u, 1 - k, part],
            device_id={"region": (down, up)[k]}, device_id_type=MESH,
        )

    def plan_copy(u, d):
        return pltpu.make_async_remote_copy(
            src_ref=pbuf.at[u, me], dst_ref=pbuf.at[u, me],
            send_sem=psend_sem.at[u, d], recv_sem=precv_sem.at[u, me],
            device_id={"scen": lax.rem(me + d, peers)}, device_id_type=MESH,
        )

    def plan_arrival(u, d):
        src = lax.rem(me + d, peers)
        return pltpu.make_async_remote_copy(
            src_ref=pbuf.at[u, src], dst_ref=pbuf.at[u, src],
            send_sem=psend_sem.at[u, d], recv_sem=precv_sem.at[u, src],
            device_id={"scen": src}, device_id_type=MESH,
        )

    def put_split(value, at, width):
        count = value.shape[0]
        high = value.astype(jnp.bfloat16)
        split[:count, at:at + width] = high
        split[count:2 * count, at:at + width] = (value - high.astype(jnp.float32)).astype(jnp.bfloat16)

    def select(weights, n, count):
        both = jnp.dot(split[:2 * count], weights[:, n * TILE:(n + 1) * TILE], preferred_element_type=jnp.float32)
        return both[:count] + both[count:]

    per_side = slots // TILE

    def split_state(c):
        for n in range(tiles):
            put_split(st[c, :, :, n * TILE:(n + 1) * TILE].reshape(rows, TILE), n * TILE, TILE)

    def gather_ties(u, k):
        for at in range(per_side):
            snd[u, k, :, at * TILE:(at + 1) * TILE] = select(pick, k * per_side + at, rows)

    def send_ties(u, sides):
        for part in range(PARTS):
            for k in sides:
                tie_copy(u, k, part).start()

    def send_plan(u):
        for d in range(1, peers):
            plan_copy(u, d).start()

    def enter():
        pl.semaphore_wait(barrier, 3 + lax.div(place_z + last_z, last_z + 1) + lax.div(2 * last_z - place_z, last_z + 1))

    def greet_far():
        @pl.when(place_z == last_z)
        def _():
            pl.semaphore_signal(token.at[1], inc=1, device_id=lower, device_id_type=MESH)

        @pl.when(place_z > 0)
        def _():
            pl.semaphore_wait(token.at[0], 1)

        @pl.when(place_z < last_z)
        def _():
            pl.semaphore_signal(token.at[0], inc=1, device_id=higher, device_id_type=MESH)
            pl.semaphore_wait(token.at[1], 1)

        @pl.when((place_z > 0) & (place_z < last_z))
        def _():
            pl.semaphore_signal(token.at[1], inc=1, device_id=lower, device_id_type=MESH)

    def start_chunk(c, peeled):
        load(0, s0_hbm, st, c).wait()
        split_state(c)
        for k in range(2):
            if k == 1 and peeled:
                build_pick(1)
            gather_ties(c, k)
            if k == 0 and peeled:
                enter()
            send_ties(c, (k,))
        pbuf[c, me] = jnp.sum(st[c], axis=0)

    start_chunk(0, True)
    pl.loop(1, chunks)(lambda c: start_chunk(c, False))

    for k in range(2):
        column = jnp.transpose(jnp.broadcast_to(tie_index[k:k + 1, :].astype(jnp.float32), (LANES, slots))).astype(jnp.int32)
        alive = lax.broadcasted_iota(jnp.int32, (slots, LANES), 0) < tie_len[0, k]
        for b in range(buses // LANES):
            ids = lax.broadcasted_iota(jnp.int32, (slots, LANES), 1) + b * LANES
            hot = one_hot((ids == column) & alive)
            place[k * slots:(k + 1) * slots, b * LANES:(b + 1) * LANES] = hot.astype(jnp.bfloat16)
            part = jnp.broadcast_to(jnp.sum(hot, axis=0, keepdims=True), (SUB, LANES))
            if k == 0:
                mrow[:, b * LANES:(b + 1) * LANES] = part
            else:
                mrow[:, b * LANES:(b + 1) * LANES] += part
    arow[...] = 1.0 - step_rate * (tie_weight * mrow[...] + day_weight)
    gens = gen_bus.shape[1]
    column = jnp.transpose(jnp.broadcast_to(gen_bus[...].astype(jnp.float32), (LANES, gens))).astype(jnp.int32)
    caps = jnp.transpose(jnp.broadcast_to(gen_cap[...], (LANES, gens)))
    for b in range(buses // LANES):
        ids = lax.broadcasted_iota(jnp.int32, (gens, LANES), 1) + b * LANES
        part = jnp.sum(jnp.where(ids == column, caps, 0.0), axis=0, keepdims=True)
        urow[:, b * LANES:(b + 1) * LANES] = jnp.broadcast_to(part, (SUB, LANES))
    greet_far()
    pl.loop(0, chunks)(send_plan)
    mat_copy.wait()

    def prepare(sweep, u, c):
        for d in range(1, peers):
            plan_arrival(u, d).wait_recv()
        plan = pbuf[u, 0]
        for src in range(1, peers):
            plan = plan + pbuf[u, src]
        plan = plan / total_scen
        if sweep == SWEEPS - 1:
            plan_out[c] = plan
        for n in range(tiles):
            cols = slice(n * TILE, (n + 1) * TILE)
            now = st[c, :, :, cols]
            day = plan[:, cols]
            base = pr[c, :, :, cols]
            if sweep == 0:
                dual = now - day
                dd[c, :, :, cols] = dual
                pr[c, :, :, cols] = base + (0.5 * tie_weight) * mrow[:, cols] * now
            else:
                dual = dd[c, :, :, cols] + now - day
            kk[:, :, cols] = step_rate * (base + day_weight * (dual - day))
            rb[0, :, cols] = now.reshape(rows, TILE).astype(jnp.bfloat16)
        for n in range(tiles):
            cols = slice(n * TILE, (n + 1) * TILE)
            slope = jnp.dot(rb[0], mat[:, cols], preferred_element_type=jnp.float32).reshape(scens, SUB, TILE)
            first[:, :, cols] = arow[:, cols] * st[c, :, :, cols] - step_rate * slope - kk[:, :, cols]

    def descend(sweep, u, c, parts):
        count = rows // PARTS * len(parts)
        lines = slice(parts[0] * (rows // PARTS), parts[0] * (rows // PARTS) + count)
        some = slice(lines.start // SUB, lines.stop // SUB)
        for k in range(2):
            for part in parts:
                tie_copy(u, 1 - k, part).wait_recv()
            put_split(rcv[u, k, lines], k * slots, slots)

        def advance(n, new, step):
            cols = slice(n * TILE, (n + 1) * TILE)
            new = jnp.minimum(jnp.maximum(new, -dm[c, some, :, cols]), urow[:, cols])
            if step < STEPS - 1:
                rb[(step + 1) % 2, lines, cols] = new.reshape(count, TILE).astype(jnp.bfloat16)
            if sweep == SWEEPS - 1 and step == STEPS - 1:
                out[some, pl.ds(pl.multiple_of(c * SUB, SUB), SUB), cols] = new
            else:
                st[c, some, :, cols] = new

        for n in range(tiles):
            cols = slice(n * TILE, (n + 1) * TILE)
            theirs = select(place, n, count).reshape(count // SUB, SUB, TILE)
            if sweep == 0:
                pr[c, some, :, cols] -= (0.5 * tie_weight) * theirs
            pull = (step_rate * tie_weight) * theirs
            kk[some, :, cols] -= pull
            advance(n, first[some, :, cols] + pull, 0)
        for step in range(1, STEPS):
            for n in range(tiles):
                cols = slice(n * TILE, (n + 1) * TILE)
                slope = jnp.dot(rb[step % 2, lines], mat[:, cols], preferred_element_type=jnp.float32).reshape(count // SUB, SUB, TILE)
                advance(n, arow[:, cols] * st[c, some, :, cols] - step_rate * slope - kk[some, :, cols], step)

    every = tuple(range(PARTS))

    @pl.loop(0, chunks)
    def first_sweep(c):
        load(1, price_hbm, pr, c).wait()
        load(2, demand_hbm, dm, c).wait()
        prepare(0, c, c)
        descend(0, c, c, every)
        u = chunks + c
        pbuf[u, me] = jnp.sum(st[c] + dd[c], axis=0)
        send_plan(u)
        split_state(c)
        for k in range(2):
            gather_ties(u, k)
        send_ties(u, (0, 1))

    @pl.loop(0, chunks - 1)
    def last_sweep(c):
        prepare(1, chunks + c, c)
        descend(1, chunks + c, c, every)

    prepare(1, 2 * chunks - 1, chunks - 1)
    for part in every:
        descend(1, 2 * chunks - 1, chunks - 1, (part,))

    def finish(u, carry):
        for k in range(2):
            for part in every:
                tie_copy(u, k, part).wait_send()
        for d in range(1, peers):
            plan_copy(u, d).wait_send()
        return carry

    lax.fori_loop(0, SWEEPS * chunks, finish, 0)


def body(start_state, price, demand, sens, gen_bus, gen_cap, tie_index, tie_len):
    _, scens, hours, buses = start_state.shape
    slots = tie_index.shape[2]
    peers = lax.axis_size("scen")
    regions = lax.axis_size("region")
    chunks = hours // SUB
    rows = scens * SUB
    f32, bf16 = jnp.float32, jnp.bfloat16
    resident = pl.BlockSpec(memory_space=pltpu.VMEM)
    anywhere = pl.BlockSpec(memory_space=pl.ANY)
    whole = pltpu.VMEM((chunks, scens, SUB, buses), f32)
    final, plan = pl.pallas_call(
        functools.partial(kernel, scens * peers, regions, peers),
        out_shape=(
            pltpu.VMEM((scens, hours, buses), f32),
            pltpu.VMEM((chunks, SUB, buses), f32),
        ),
        in_specs=[anywhere] * 4 + [resident] * 3 + [pl.BlockSpec(memory_space=pltpu.SMEM)],
        out_specs=(resident, resident),
        scratch_shapes=[
            whole, whole, whole, whole,
            pltpu.VMEM((buses, buses), bf16),
            pltpu.VMEM((buses, 2 * slots), bf16),
            pltpu.VMEM((2 * slots, buses), bf16),
            pltpu.VMEM((SUB, buses), f32),
            pltpu.VMEM((SUB, buses), f32),
            pltpu.VMEM((SUB, buses), f32),
            pltpu.VMEM((2 * rows, buses), bf16),
            pltpu.VMEM((2, rows, buses), bf16),
            pltpu.VMEM((scens, SUB, buses), f32),
            pltpu.VMEM((scens, SUB, buses), f32),
            pltpu.VMEM((SWEEPS * chunks, 2, rows, slots), f32),
            pltpu.VMEM((SWEEPS * chunks, 2, rows, slots), f32),
            pltpu.VMEM((SWEEPS * chunks, peers, SUB, buses), f32),
            pltpu.SemaphoreType.REGULAR((2,)),
            pltpu.SemaphoreType.DMA((3, chunks)),
            pltpu.SemaphoreType.DMA,
            pltpu.SemaphoreType.DMA((SWEEPS * chunks, 2, PARTS)),
            pltpu.SemaphoreType.DMA((SWEEPS * chunks, 2, PARTS)),
            pltpu.SemaphoreType.DMA((SWEEPS * chunks, peers)),
            pltpu.SemaphoreType.DMA((SWEEPS * chunks, peers)),
        ],
        compiler_params=pltpu.CompilerParams(collective_id=0, has_side_effects=True),
        name="dispatch",
    )(start_state[0], price[0], demand[0], sens[0], gen_bus, gen_cap, tie_index[0], tie_len)
    return (final[None], plan.reshape(1, hours, buses))


def solution(mesh):
    in_specs = (
        P("region", "scen", None, None),
        P("region", "scen", None, None),
        P("region", "scen", None, None),
        P("region", None, None),
        P("region", None),
        P("region", None),
        P("region", None, None),
        P("region", None),
    )
    out_specs = (P("region", "scen", None, None), P("region", None, None))
    return jax.shard_map(body, mesh=mesh, in_specs=in_specs, out_specs=out_specs, check_vma=False)
```
